256 devices in a mesh: scen: 8 (over x, y_hi), rows: 32 (over z, y_lo, core).
Axes of the slice: x: 4, y: 4 (y_hi: 2, y_lo: 2; y = y_hi * 2 + y_lo), z: 8, core: 2. Of those that a mesh axis runs over, the one named last changes fastest.
Arguments:
- factor_rows: float32 [32, 16384, 1024], P('scen', 'rows'), may hold values from -1.5 to 1.5
- panel_factor: float32 [32, 1024, 512], P('scen'), may hold values from -0.03125 to 0.03125
- pivot_add: float32 [512, 512], replicated, may hold values from -1 to 4, as said below
- trailing: float32 [16384, 4096], P('rows', 'scen'), may hold values from -6 to 6
Outputs:
- panel: float32 [16384, 512], P('rows')
- updated: float32 [16384, 4096], P('rows', 'scen')
The draws below stay inside these ranges and needn't reach their ends.
Inputs may be any that keep to these rules, and one draw needn't show every extreme that they name: `pivot_add`: symmetric positive definite; its diagonal lies between 1 and 3 and its off-diagonal entries are small.
All inputs are finite; a program needn't handle non-finite values.
Results may differ from the reference program's by a relative error of at most 0.0001.
Values sent between devices are 32-bit elements; how exact they have to be, the bound alone decides.
No kernel may reach another device: no remote copies, remote signals or barrier semaphores. Data moves between devices by JAX's collectives and lax.ppermute only.
A program may use at most 128 MiB of HBM per device.

```python
import jax
import jax.numpy as jnp
from jax import lax

K = 1024
PB = 512
TC = 4096
RB = 512
SCEN = 32
NR = 16384
N_SCEN = 8
N_ROWS = 32


def draw_pivot_add(key, part):
    first_key, second_key = jax.random.split(jax.random.fold_in(key, 4711))
    diag_vals = jax.random.uniform(first_key, (PB,), jnp.float32, 1.0, 3.0)
    noise_part = jax.random.normal(second_key, (PB, PB), jnp.float32) * (0.25 / jnp.sqrt(jnp.float32(PB)))
    noise_part = noise_part + noise_part.T
    noise_part = noise_part * (1.0 - jnp.eye(PB, dtype=jnp.float32))
    return (jnp.diag(diag_vals) + noise_part).astype(jnp.float32)


def with_spikes(drawn, own_key, source, target, parts, factor):
    def block_of(position):
        return (jnp.arange(drawn.shape[position]) // (drawn.shape[position] // parts)).reshape((-1,) + (1,) * (drawn.ndim - 1 - position))

    first = jax.random.permutation(own_key, parts)[block_of(target)]
    far = (block_of(target) + parts // 2) % parts
    return jnp.where((block_of(source) == first) | (block_of(source) == far), factor * drawn, drawn)


def level_of(key, shape, shards, smallest, high):
    def one(axis_at, blocks):
        heights = jax.random.uniform(jax.random.fold_in(jax.random.fold_in(key, 6), axis_at), (blocks,), jnp.float32, smallest / len(shards), high / len(shards))
        return jnp.repeat(jnp.exp(heights), shape[axis_at] // blocks).reshape((-1,) + (1,) * (len(shape) - axis_at - 1))

    loudness = one(*shards[0])
    for cut in shards[1:]:
        loudness = loudness * one(*cut)
    return loudness


def bell_draw(rng, shape, scale, limit, shards=(), kind=jnp.bfloat16):
    entries = scale * jax.random.normal(rng, shape, jnp.float32)
    if shards:
        entries = entries * level_of(rng, shape, shards, -0.22, 0.18)
    return jnp.clip(entries, -limit, limit).astype(kind)


def bell_draw_with(stream_key, extent, scale, limit, cuts, heavy, kind=jnp.bfloat16):
    entries = scale * jax.random.normal(stream_key, extent, jnp.float32)
    if cuts:
        entries = entries * level_of(stream_key, extent, cuts, -0.22, 0.18)
    return jnp.clip(with_spikes(entries, jax.random.fold_in(stream_key, 3), *heavy), -limit, limit).astype(kind)


def setup_inputs(seed: int = 0) -> dict:
    arg_keys = jax.random.split(jax.random.key(seed), 5)
    return {
        "factor_rows": bell_draw_with(arg_keys[0], (SCEN, NR, K), 0.25, 1.5, ((0, 8), (1, 32)), (0, 1, 32, 2.75), jnp.float32),
        "panel_factor": bell_draw(arg_keys[1], (SCEN, K, PB), (SCEN * K) ** -0.5, 0.03125, ((0, 8),), jnp.float32),
        "pivot_add": draw_pivot_add(jax.random.fold_in(arg_keys[4], 71), 0),
        "trailing": bell_draw(arg_keys[3], (NR, TC), 1.0, 6.0, ((0, 32), (1, 8)), jnp.float32),
    }


exact_mode = lax.Precision.HIGHEST

def reference(factor_rows, panel_factor, pivot_add, trailing):
    stacked = panel_factor.reshape(SCEN * K, PB)
    pivot_block = lax.dot_general(stacked.astype(jnp.float32), stacked.astype(jnp.float32), (((0,), (0,)), ((), ())), precision=exact_mode, preferred_element_type=jnp.float32) + pivot_add

    def add_group(group, total):
        return total + jnp.dot(factor_rows[group].astype(jnp.float32), panel_factor[group].astype(jnp.float32), precision=exact_mode, preferred_element_type=jnp.float32)
    slab = lax.fori_loop(0, SCEN, add_group, jnp.zeros((NR, PB), jnp.float32))
    factor_chol = jnp.linalg.cholesky(pivot_block)
    panel = lax.linalg.triangular_solve(factor_chol, slab, left_side=False, lower=True, transpose_a=True)
    tile_width = TC // (N_ROWS * N_SCEN)
    picked = panel.reshape(N_ROWS, N_SCEN, RB // N_SCEN, PB)[:, :, :tile_width, :]
    cross = jnp.transpose(picked, (1, 0, 2, 3)).reshape(TC, PB)
    product = jnp.dot(panel.astype(jnp.float32), cross.T.astype(jnp.float32), precision=exact_mode, preferred_element_type=jnp.float32)
    return (panel, trailing - product)
```

```python
import jax
import jax.numpy as jnp
from jax import lax
from jax.experimental import pallas as pl
from jax.experimental.pallas import tpu as pltpu
from jax.sharding import PartitionSpec as P


N = 512
B = 128
EXACT = lax.Precision.HIGHEST
SPLIT = lax.Precision.HIGH
VMEM = pl.BlockSpec(memory_space=pltpu.VMEM)
SMEM = pl.BlockSpec(memory_space=pltpu.SMEM)


def spread(x):
    return jnp.broadcast_to(x, (8, 128))


def factor_block(sv, ev):
    sub = lax.broadcasted_iota(jnp.int32, (8, 128), 0)
    for b in range(16):
        col = {v: [spread(sv[v][:, 8 * b + i : 8 * b + i + 1]) for i in range(8)] for v in range(b, 16)}
        trow = [spread(sv[b][i : i + 1, :]) for i in range(8)]
        frow = [spread(ev[b][i : i + 1, :]) for i in range(8)]
        el = [[spread(col[b][j][i : i + 1, :]) for j in range(i + 1)] for i in range(8)]
        low = [[None] * 8 for _ in range(8)]
        inv = [None] * 8
        for j in range(8):
            inv[j] = lax.rsqrt(el[j][j])
            for i in range(j + 1, 8):
                low[i][j] = el[i][j] * inv[j]
            for i in range(j + 1, 8):
                for m in range(j + 1, i + 1):
                    el[i][m] = el[i][m] - low[i][j] * low[m][j]
            trow[j] = trow[j] * inv[j]
            frow[j] = frow[j] * inv[j]
            for i in range(j + 1, 8):
                trow[i] = trow[i] - low[i][j] * trow[j]
                frow[i] = frow[i] - low[i][j] * frow[j]
        for v in range(b + 1, 16):
            c = col[v]
            for j in range(8):
                c[j] = c[j] * inv[j]
                for i in range(j + 1, 8):
                    c[i] = c[i] - low[i][j] * c[j]
            for j in range(8):
                sv[v] = sv[v] - c[j] * trow[j]
                ev[v] = ev[v] - c[j] * frow[j]
        out = frow[0]
        for i in range(1, 8):
            out = jnp.where(sub == i, frow[i], out)
        ev[b] = out
    return ev


def dot(a, b, ca, cb):
    return lax.dot_general(a, b, (((ca,), (cb,)), ((), ())), precision=EXACT, preferred_element_type=jnp.float32)


def halves(a):
    hi = a.astype(jnp.bfloat16)
    return hi, (a - hi.astype(jnp.float32)).astype(jnp.bfloat16)


def dot3(a, b, ca, cb):
    def one(x, y):
        return lax.dot_general(x, y, (((ca,), (cb,)), ((), ())), preferred_element_type=jnp.float32)

    return one(a[0], b[0]) + (one(a[0], b[1]) + one(a[1], b[0]))


def factor_kernel(pos_ref, mine_ref, other_ref, add_ref, m_ref, s_ref):
    s = pos_ref[0]
    c = pos_ref[1]
    for half, ref in ((c, mine_ref), (1 - c, other_ref)):
        for k in range(8):
            at = pl.ds(pl.multiple_of(256 * half + 32 * (s ^ k), 32), 32)
            s_ref[at, :] = ref[32 * k : 32 * k + 32, :] + add_ref[at, :]
    rows = lax.broadcasted_iota(jnp.int32, (8, 128), 0)
    lanes = lax.broadcasted_iota(jnp.int32, (8, 128), 1)
    m_ref[...] = jnp.zeros((N, N), jnp.float32)
    for k in range(4):
        lo = B * k
        hi = lo + B
        sv = [s_ref[lo + 8 * v : lo + 8 * v + 8, lo:hi] for v in range(16)]
        ev = [jnp.where(lanes == rows + 8 * v, 1.0, 0.0).astype(jnp.float32) for v in range(16)]
        mk = jnp.concatenate(factor_block(sv, ev), axis=0)
        if k:
            m_ref[lo:hi, :lo] = dot(mk, m_ref[lo:hi, :lo], 1, 0)
        m_ref[lo:hi, lo:hi] = mk
        if k < 3:
            p = dot(s_ref[hi:, lo:hi], mk, 1, 1)
            s_ref[hi:, hi:] = s_ref[hi:, hi:] - dot(p, p, 1, 1)
            m_ref[hi:, :hi] = m_ref[hi:, :hi] - dot(p, m_ref[lo:hi, :hi], 1, 0)


def update_kernel(pos_ref, m_ref, trail_ref, *refs):
    slab_refs, cross_refs = refs[:8], refs[8:11]
    panel_ref, out_ref, x_ref = refs[11:]
    s = pos_ref[0]
    c = pos_ref[1]
    y = pos_ref[2]
    z = pos_ref[3]
    for k in range(8):
        x_ref[pl.ds(pl.multiple_of(64 * (s ^ k), 64), 64), :] = slab_refs[k][...]
    for q in range(4):
        for j in range(8):
            r = ((z - j) & 7) * 4 + (y ^ (q & 1)) * 2 + (c ^ (q >> 1))
            at = pl.ds(pl.multiple_of(N + 16 * r, 16), 16)
            if q < 2:
                x_ref[at, :] = cross_refs[q][16 * j : 16 * j + 16, :]
            else:
                first = 128 * (q - 2) + 16 * j
                x_ref[at, :] = cross_refs[2][first : first + 16, :]
    solved = dot3(halves(x_ref[...]), halves(m_ref[...]), 1, 1)
    panel = solved[:N]
    panel_ref[...] = panel
    out_ref[...] = trail_ref[...] - dot3(halves(panel), halves(solved[N:]), 1, 1)


def square(n):
    return jax.ShapeDtypeStruct((n, N), jnp.float32)


def trade(chunks, where):
    got = [chunks[0]]
    for k in range(1, 8):
        got.append(lax.ppermute(chunks[k], "scen", [(i, i ^ k) for i in range(8)]))
    return got


def per_device(factor_rows, panel_factor, pivot_add, trailing):
    groups, depth, width = panel_factor.shape
    s = lax.axis_index("scen")
    r = lax.axis_index("rows")
    core = r & 1
    pos = jnp.stack([s, core, (r >> 1) & 1, r >> 2]).astype(jnp.int32)
    tall = panel_factor.reshape(groups * depth, width)
    gram = lax.dot_general(
        lax.dynamic_slice_in_dim(tall, core * 256, 256, 1),
        tall,
        (((0,), (0,)), ((), ())),
        precision=SPLIT,
        preferred_element_type=jnp.float32,
    )
    parts = [lax.dynamic_slice_in_dim(gram, (s ^ k) * 32, 32, 0) for k in range(8)]
    mine = sum(trade(parts, "gram"))
    mine = jnp.concatenate(trade([mine] * 8, "gram"), axis=0)
    other = lax.ppermute(mine, "rows", [(i, i ^ 1) for i in range(32)])
    m = pl.pallas_call(
        factor_kernel,
        out_shape=square(N),
        in_specs=[SMEM, VMEM, VMEM, VMEM],
        out_specs=VMEM,
        scratch_shapes=[pltpu.VMEM((N, N), jnp.float32)],
        compiler_params=pltpu.CompilerParams(vmem_limit_bytes=12 << 20),
        name="factor",
    )(pos, mine, other, pivot_add)

    slab = jnp.einsum("grk,gkp->rp", factor_rows, panel_factor, precision=SPLIT, preferred_element_type=jnp.float32)
    parts = [lax.dynamic_slice_in_dim(slab, (s ^ k) * 64, 64, 0) for k in range(8)]
    own = sum(trade(parts, "slab"))
    pieces = trade([own] * 8, "slab")
    near = [own[:16]]
    for j in range(1, 8):
        near.append(lax.ppermute(own[:16], "rows", [(i, ((i // 4 + j) % 8) * 4 + i % 4) for i in range(32)]))
    near = jnp.concatenate(near, axis=0)
    beside = lax.ppermute(near, "rows", [(i, i ^ 2) for i in range(32)])
    across = lax.ppermute(jnp.concatenate([near, beside], axis=0), "rows", [(i, i ^ 1) for i in range(32)])

    return pl.pallas_call(
        update_kernel,
        out_shape=(square(N), square(N)),
        in_specs=[SMEM] + [VMEM] * 13,
        out_specs=(VMEM, VMEM),
        scratch_shapes=[pltpu.VMEM((2 * N, N), jnp.float32)],
        compiler_params=pltpu.CompilerParams(vmem_limit_bytes=28 << 20),
        name="update",
    )(pos, m, trailing, *pieces, near, beside, across)


def solution(mesh):
    return jax.shard_map(
        per_device,
        mesh=mesh,
        in_specs=(P("scen", "rows", None), P("scen", None, None), P(), P("rows", "scen")),
        out_specs=(P("rows", None), P("rows", "scen")),
        check_vma=False,
    )
```

```python
import jax
import jax.numpy as jnp
from jax import lax
from jax.experimental import pallas as pl
from jax.experimental.pallas import tpu as pltpu
from jax.sharding import PartitionSpec as P


N = 512
B = 128
EXACT = lax.Precision.HIGHEST
VMEM = pl.BlockSpec(memory_space=pltpu.VMEM)
SMEM = pl.BlockSpec(memory_space=pltpu.SMEM)


def spread(x):
    return jnp.broadcast_to(x, (8, 128))


def factor_block(sv, ev):
    sub = lax.broadcasted_iota(jnp.int32, (8, 128), 0)
    for b in range(16):
        col = {v: [spread(sv[v][:, 8 * b + i : 8 * b + i + 1]) for i in range(8)] for v in range(b, 16)}
        trow = [spread(sv[b][i : i + 1, :]) for i in range(8)]
        frow = [spread(ev[b][i : i + 1, :]) for i in range(8)]
        el = [[spread(col[b][j][i : i + 1, :]) for j in range(i + 1)] for i in range(8)]
        low = [[None] * 8 for _ in range(8)]
        inv = [None] * 8
        for j in range(8):
            inv[j] = lax.rsqrt(el[j][j])
            for i in range(j + 1, 8):
                low[i][j] = el[i][j] * inv[j]
            for i in range(j + 1, 8):
                for m in range(j + 1, i + 1):
                    el[i][m] = el[i][m] - low[i][j] * low[m][j]
            trow[j] = trow[j] * inv[j]
            frow[j] = frow[j] * inv[j]
            for i in range(j + 1, 8):
                trow[i] = trow[i] - low[i][j] * trow[j]
                frow[i] = frow[i] - low[i][j] * frow[j]
        for v in range(b + 1, 16):
            c = col[v]
            for j in range(8):
                c[j] = c[j] * inv[j]
                for i in range(j + 1, 8):
                    c[i] = c[i] - low[i][j] * c[j]
            for j in range(8):
                sv[v] = sv[v] - c[j] * trow[j]
                ev[v] = ev[v] - c[j] * frow[j]
        out = frow[0]
        for i in range(1, 8):
            out = jnp.where(sub == i, frow[i], out)
        ev[b] = out
    return ev


def dot(a, b, ca, cb):
    return lax.dot_general(a, b, (((ca,), (cb,)), ((), ())), precision=EXACT, preferred_element_type=jnp.float32)


def halves(a):
    hi = a.astype(jnp.bfloat16)
    return hi, (a - hi.astype(jnp.float32)).astype(jnp.bfloat16)


def dot3(a, b, ca, cb):
    def one(x, y):
        return lax.dot_general(x, y, (((ca,), (cb,)), ((), ())), preferred_element_type=jnp.float32)

    return one(a[0], b[0]) + (one(a[0], b[1]) + one(a[1], b[0]))


def gram_kernel(pos_ref, p_ref, out_ref, acc_ref):
    piece = pos_ref[0] & 7

    @pl.when(pl.program_id(0) == 0)
    def _():
        acc_ref[...] = jnp.zeros(acc_ref.shape, jnp.float32)

    wide = halves(p_ref[0])
    part = halves(p_ref[0, :, pl.ds(pl.multiple_of(128 * (piece >> 1), 128), 128)])
    acc_ref[...] += dot3(part, wide, 0, 0)

    @pl.when(pl.program_id(0) == pl.num_programs(0) - 1)
    def _():
        out_ref[...] = acc_ref[pl.ds(pl.multiple_of(64 * (piece & 1), 64), 64), :]


def slab_kernel(f_ref, p_ref, out_ref):
    @pl.when((pl.program_id(0) == 0) & (pl.program_id(1) == 0))
    def _():
        out_ref[...] = jnp.zeros(out_ref.shape, jnp.float32)

    out_ref[...] += dot3(halves(f_ref[0]), halves(p_ref[0]), 1, 0)


def factor_kernel(pos_ref, *refs):
    add_ref, m_ref, s_ref = refs[8:]
    for k in range(8):
        at = pl.ds(pl.multiple_of(64 * ((pos_ref[0] & 7) ^ k), 64), 64)
        s_ref[at, :] = refs[k][...] + add_ref[at, :]
    rows = lax.broadcasted_iota(jnp.int32, (8, 128), 0)
    lanes = lax.broadcasted_iota(jnp.int32, (8, 128), 1)
    m_ref[...] = jnp.zeros((N, N), jnp.float32)
    for k in range(4):
        lo = B * k
        hi = lo + B
        sv = [s_ref[lo + 8 * v : lo + 8 * v + 8, lo:hi] for v in range(16)]
        ev = [jnp.where(lanes == rows + 8 * v, 1.0, 0.0).astype(jnp.float32) for v in range(16)]
        mk = jnp.concatenate(factor_block(sv, ev), axis=0)
        if k:
            m_ref[lo:hi, :lo] = dot(mk, m_ref[lo:hi, :lo], 1, 0)
        m_ref[lo:hi, lo:hi] = mk
        if k < 3:
            p = dot(s_ref[hi:, lo:hi], mk, 1, 1)
            s_ref[hi:, hi:] = s_ref[hi:, hi:] - dot(p, p, 1, 1)
            m_ref[hi:, :hi] = m_ref[hi:, :hi] - dot(p, m_ref[lo:hi, :hi], 1, 0)


def update_kernel(pos_ref, m_ref, trail_ref, slab_ref, *refs):
    panel_ref, out_ref, x_ref = refs[4:]
    for q in range(4):
        for z in range(8):
            at = pl.ds(pl.multiple_of(16 * (4 * z + ((pos_ref[0] & 3) ^ q)), 16), 16)
            x_ref[at, :] = refs[q][16 * z : 16 * z + 16, :]
    inv = halves(m_ref[...])
    panel = dot3(halves(slab_ref[...]), inv, 1, 1)
    panel_ref[...] = panel
    cross = dot3(halves(x_ref[...]), inv, 1, 1)
    out_ref[...] = trail_ref[...] - dot3(halves(panel), halves(cross), 1, 1)


def shape(n):
    return jax.ShapeDtypeStruct((n, N), jnp.float32)


def swap(x, axis, groups=None):
    return lax.all_to_all(x, axis, split_axis=0, concat_axis=0, axis_index_groups=groups, tiled=True)


def gathered(x, axis, groups=None):
    return swap(jnp.broadcast_to(x[None], (8, *x.shape)), axis, groups).reshape(-1, N)


def flip(x, axis, bits):
    n = lax.axis_size(axis)
    return lax.ppermute(x, axis, [(i, i ^ bits) for i in range(n)])


def per_device(factor_rows, panel_factor, pivot_add, trailing):
    groups, depth, _ = panel_factor.shape
    pos = lax.axis_index("rows").astype(jnp.int32).reshape(1)
    gram = pl.pallas_call(
        gram_kernel,
        grid=(groups,),
        out_shape=shape(64),
        in_specs=[SMEM, pl.BlockSpec((1, depth, N), lambda g: (g, 0, 0))],
        out_specs=pl.BlockSpec((64, N), lambda g: (0, 0)),
        scratch_shapes=[pltpu.VMEM((128, N), jnp.float32)],
        compiler_params=pltpu.CompilerParams(vmem_limit_bytes=56 << 20),
        name="gram",
    )(pos, panel_factor)
    slab = pl.pallas_call(
        slab_kernel,
        grid=(groups, depth // 512),
        out_shape=shape(N),
        in_specs=[
            pl.BlockSpec((1, N, 512), lambda g, k: (g, 0, k)),
            pl.BlockSpec((1, 512, N), lambda g, k: (g, k, 0)),
        ],
        out_specs=pl.BlockSpec((N, N), lambda g, k: (0, 0)),
        compiler_params=pltpu.CompilerParams(vmem_limit_bytes=56 << 20),
        name="slab",
    )(factor_rows, panel_factor)

    own = swap(slab.reshape(8, 64, N), "scen")
    own = own.sum(0)
    gram = gram + flip(gram, "scen", 1)
    gram = (gram + flip(gram, "scen", 2)) + (flip(gram, "scen", 4) + flip(gram, "scen", 6))
    near = [gram]
    for b in (2, 4, 6):
        near.append(flip(gram, "rows", b))
    far = [flip(x, "rows", 1) for x in near]
    pieces = [x for pair in zip(near, far) for x in pair]
    m = pl.pallas_call(
        factor_kernel,
        out_shape=shape(N),
        in_specs=[SMEM] + [VMEM] * 9,
        out_specs=VMEM,
        scratch_shapes=[pltpu.VMEM((N, N), jnp.float32)],
        compiler_params=pltpu.CompilerParams(vmem_limit_bytes=12 << 20),
        name="factor",
    )(pos, *pieces, pivot_add)

    column = [[4 * z + k for z in range(8)] for k in range(4)]
    cross = [gathered(own[:16], "rows", column)]
    cross.append(flip(cross[0], "rows", 1))
    cross += [flip(cross[0], "rows", 2)]
    cross.append(flip(cross[2], "rows", 1))
    whole = gathered(own, "scen")
    return pl.pallas_call(
        update_kernel,
        out_shape=(shape(N), shape(N)),
        in_specs=[SMEM] + [VMEM] * 7,
        out_specs=(VMEM, VMEM),
        scratch_shapes=[pltpu.VMEM((N, N), jnp.float32)],
        compiler_params=pltpu.CompilerParams(vmem_limit_bytes=28 << 20),
        name="update",
    )(pos, m, trailing, whole, *cross)


def solution(mesh):
    return jax.shard_map(
        per_device,
        mesh=mesh,
        in_specs=(P("scen", "rows", None), P("scen", None, None), P(), P("rows", "scen")),
        out_specs=(P("rows", None), P("rows", "scen")),
        check_vma=False,
    )
```

```python
import jax
import jax.numpy as jnp
from jax import lax
from jax.experimental import pallas as pl
from jax.experimental.pallas import tpu as pltpu
from jax.sharding import PartitionSpec as P


N = 512
B = 128
EXACT = lax.Precision.HIGHEST
VMEM = pl.BlockSpec(memory_space=pltpu.VMEM)
HBM = pl.BlockSpec(memory_space=pltpu.HBM)
SMEM = pl.BlockSpec(memory_space=pltpu.SMEM)


def spread(x):
    return jnp.broadcast_to(x, (8, 128))


def factor_block(sv, ev):
    sub = lax.broadcasted_iota(jnp.int32, (8, 128), 0)
    for b in range(16):
        col = {v: [spread(sv[v][:, 8 * b + i : 8 * b + i + 1]) for i in range(8)] for v in range(b, 16)}
        trow = [spread(sv[b][i : i + 1, :]) for i in range(8)]
        frow = [spread(ev[b][i : i + 1, :]) for i in range(8)]
        el = [[spread(col[b][j][i : i + 1, :]) for j in range(i + 1)] for i in range(8)]
        low = [[None] * 8 for _ in range(8)]
        inv = [None] * 8
        for j in range(8):
            inv[j] = lax.rsqrt(el[j][j])
            for i in range(j + 1, 8):
                low[i][j] = el[i][j] * inv[j]
            for i in range(j + 1, 8):
                for m in range(j + 1, i + 1):
                    el[i][m] = el[i][m] - low[i][j] * low[m][j]
            trow[j] = trow[j] * inv[j]
            frow[j] = frow[j] * inv[j]
            for i in range(j + 1, 8):
                trow[i] = trow[i] - low[i][j] * trow[j]
                frow[i] = frow[i] - low[i][j] * frow[j]
        for v in range(b + 1, 16):
            c = col[v]
            for j in range(8):
                c[j] = c[j] * inv[j]
                for i in range(j + 1, 8):
                    c[i] = c[i] - low[i][j] * c[j]
            for j in range(8):
                sv[v] = sv[v] - c[j] * trow[j]
                ev[v] = ev[v] - c[j] * frow[j]
        out = frow[0]
        for i in range(1, 8):
            out = jnp.where(sub == i, frow[i], out)
        ev[b] = out
    return ev


def dot(a, b, ca, cb):
    return lax.dot_general(a, b, (((ca,), (cb,)), ((), ())), precision=EXACT, preferred_element_type=jnp.float32)


def halves(a):
    hi = a.astype(jnp.bfloat16)
    return hi, (a - hi.astype(jnp.float32)).astype(jnp.bfloat16)


def dot3(a, b, ca, cb):
    def one(x, y):
        return lax.dot_general(x, y, (((ca,), (cb,)), ((), ())), preferred_element_type=jnp.float32)

    return one(a[0], b[0]) + (one(a[0], b[1]) + one(a[1], b[0]))


def product_kernel(pos_ref, f_ref, p_ref, slab_ref, gram_ref, acc_ref):
    piece = pos_ref[0] & 7

    @pl.when(pl.program_id(0) == 0)
    def _():
        acc_ref[...] = jnp.zeros(acc_ref.shape, jnp.float32)

    part = p_ref[0, :, pl.ds(pl.multiple_of(128 * (piece >> 1), 128), 128)].T
    acc_ref[...] += dot3(halves(jnp.concatenate([f_ref[0], part], axis=0)), halves(p_ref[0]), 1, 0)

    @pl.when(pl.program_id(0) == pl.num_programs(0) - 1)
    def _():
        slab_ref[...] = acc_ref[:N]
        gram_ref[...] = acc_ref[pl.ds(pl.multiple_of(N + 64 * (piece & 1), 64), 64), :]


def factor_kernel(pos_ref, *refs):
    add_hbm, m_ref, s_ref, add_ref, sems = refs[8:]
    copies = [pltpu.make_async_copy(add_hbm, add_ref, sems.at[8])]
    for k in range(8):
        at = pl.ds(pl.multiple_of(64 * ((pos_ref[0] & 7) ^ k), 64), 64)
        copies.append(pltpu.make_async_copy(refs[k], s_ref.at[at, :], sems.at[k]))
    for copy in copies:
        copy.start()
    for copy in copies:
        copy.wait()
    s_ref[...] = s_ref[...] + add_ref[...]
    rows = lax.broadcasted_iota(jnp.int32, (8, 128), 0)
    lanes = lax.broadcasted_iota(jnp.int32, (8, 128), 1)
    m_ref[...] = jnp.zeros((N, N), jnp.float32)
    for k in range(4):
        lo = B * k
        hi = lo + B
        sv = [s_ref[lo + 8 * v : lo + 8 * v + 8, lo:hi] for v in range(16)]
        ev = [jnp.where(lanes == rows + 8 * v, 1.0, 0.0).astype(jnp.float32) for v in range(16)]
        mk = jnp.concatenate(factor_block(sv, ev), axis=0)
        if k:
            m_ref[lo:hi, :lo] = dot(mk, m_ref[lo:hi, :lo], 1, 0)
        m_ref[lo:hi, lo:hi] = mk
        if k < 3:
            p = dot(s_ref[hi:, lo:hi], mk, 1, 1)
            s_ref[hi:, hi:] = s_ref[hi:, hi:] - dot(p, p, 1, 1)
            m_ref[hi:, :hi] = m_ref[hi:, :hi] - dot(p, m_ref[lo:hi, :hi], 1, 0)


def update_kernel(pos_ref, m_hbm, trail_hbm, slab_hbm, *refs):
    panel_ref, out_ref, m_ref, slab_ref, x_ref, trail_ref, sems = refs[4:]
    copies = [pltpu.make_async_copy(slab_hbm, slab_ref, sems.at[4]), pltpu.make_async_copy(m_hbm, m_ref, sems.at[6])]
    for q in range(4):
        copies.append(pltpu.make_async_copy(refs[q], x_ref.at[:, (pos_ref[0] & 3) ^ q], sems.at[q]))
    copies.append(pltpu.make_async_copy(trail_hbm, trail_ref, sems.at[5]))
    for copy in copies:
        copy.start()
    for copy in copies:
        copy.wait()
    inv = halves(m_ref[...])
    panel = dot3(halves(slab_ref[...]), inv, 1, 1)
    panel_ref[...] = panel
    cross = dot3(halves(x_ref[...].reshape(N, N)), inv, 1, 1)
    out_ref[...] = trail_ref[...] - dot3(halves(panel), halves(cross), 1, 1)


def shape(n):
    return jax.ShapeDtypeStruct((n, N), jnp.float32)


def swap(x, axis, groups=None):
    return lax.all_to_all(x, axis, split_axis=0, concat_axis=0, axis_index_groups=groups, tiled=True)


def gathered(x, axis, groups=None):
    return swap(jnp.broadcast_to(x[None], (8, *x.shape)), axis, groups).reshape(-1, N)


def flip(x, axis, bits):
    n = lax.axis_size(axis)
    return lax.ppermute(x, axis, [(i, i ^ bits) for i in range(n)])


def per_device(factor_rows, panel_factor, pivot_add, trailing):
    groups, depth, _ = panel_factor.shape
    pos = lax.axis_index("rows").astype(jnp.int32).reshape(1)
    slab, gram = pl.pallas_call(
        product_kernel,
        grid=(groups,),
        out_shape=(shape(N), shape(64)),
        in_specs=[
            SMEM,
            pl.BlockSpec((1, N, depth), lambda g: (g, 0, 0)),
            pl.BlockSpec((1, depth, N), lambda g: (g, 0, 0)),
        ],
        out_specs=(pl.BlockSpec((N, N), lambda g: (0, 0)), pl.BlockSpec((64, N), lambda g: (0, 0))),
        scratch_shapes=[pltpu.VMEM((N + 128, N), jnp.float32)],
        compiler_params=pltpu.CompilerParams(vmem_limit_bytes=56 << 20),
        name="product",
    )(pos, factor_rows, panel_factor)

    own = swap(slab.reshape(8, 64, N), "scen")
    own = own.sum(0)
    gram = gram + flip(gram, "scen", 1)
    gram = (gram + flip(gram, "scen", 2)) + (flip(gram, "scen", 4) + flip(gram, "scen", 6))
    near = [gram]
    for b in (2, 4, 6):
        near.append(flip(gram, "rows", b))
    far = [flip(x, "rows", 1) for x in near]
    pieces = [x for pair in zip(near, far) for x in pair]
    m = pl.pallas_call(
        factor_kernel,
        out_shape=shape(N),
        in_specs=[SMEM] + [HBM] * 9,
        out_specs=VMEM,
        scratch_shapes=[pltpu.VMEM((N, N), jnp.float32)] * 2 + [pltpu.SemaphoreType.DMA((9,))],
        name="factor",
    )(pos, *pieces, pivot_add)

    column = [[4 * z + k for z in range(8)] for k in range(4)]
    cross = [gathered(own[:16], "rows", column)]
    cross += [flip(cross[0], "rows", q) for q in (1, 2, 3)]
    whole = gathered(own, "scen")
    return pl.pallas_call(
        update_kernel,
        out_shape=(shape(N), shape(N)),
        in_specs=[SMEM] + [HBM] * 7,
        out_specs=(VMEM, VMEM),
        scratch_shapes=[
            pltpu.VMEM((N, N), jnp.float32),
            pltpu.VMEM((N, N), jnp.float32),
            pltpu.VMEM((8, 4, 16, N), jnp.float32),
            pltpu.VMEM((N, N), jnp.float32),
            pltpu.SemaphoreType.DMA((7,)),
        ],
        compiler_params=pltpu.CompilerParams(vmem_limit_bytes=28 << 20),
        name="update",
    )(pos, m, trailing, whole, *[x.reshape(8, 16, N) for x in cross])


def solution(mesh):
    return jax.shard_map(
        per_device,
        mesh=mesh,
        in_specs=(P("scen", "rows", None), P("scen", None, None), P(), P("rows", "scen")),
        out_specs=(P("rows", None), P("rows", "scen")),
        check_vma=False,
    )
```

```python
import jax
import jax.numpy as jnp
from jax import lax
from jax.experimental import pallas as pl
from jax.experimental.pallas import tpu as pltpu
from jax.sharding import PartitionSpec as P


N = 512
B = 128
EXACT = lax.Precision.HIGHEST
VMEM = pl.BlockSpec(memory_space=pltpu.VMEM)
HBM = pl.BlockSpec(memory_space=pltpu.HBM)
SMEM = pl.BlockSpec(memory_space=pltpu.SMEM)


def spread(x):
    return jnp.broadcast_to(x, (8, 128))


def factor_block(sv, ev):
    sub = lax.broadcasted_iota(jnp.int32, (8, 128), 0)
    for b in range(16):
        col = {v: [spread(sv[v][:, 8 * b + i : 8 * b + i + 1]) for i in range(8)] for v in range(b, 16)}
        trow = [spread(sv[b][i : i + 1, :]) for i in range(8)]
        frow = [spread(ev[b][i : i + 1, :]) for i in range(8)]
        el = [[spread(col[b][j][i : i + 1, :]) for j in range(i + 1)] for i in range(8)]
        low = [[None] * 8 for _ in range(8)]
        inv = [None] * 8
        for j in range(8):
            inv[j] = lax.rsqrt(el[j][j])
            for i in range(j + 1, 8):
                low[i][j] = el[i][j] * inv[j]
            for i in range(j + 1, 8):
                for m in range(j + 1, i + 1):
                    el[i][m] = el[i][m] - low[i][j] * low[m][j]
            trow[j] = trow[j] * inv[j]
            frow[j] = frow[j] * inv[j]
            for i in range(j + 1, 8):
                trow[i] = trow[i] - low[i][j] * trow[j]
                frow[i] = frow[i] - low[i][j] * frow[j]
        for v in range(b + 1, 16):
            c = col[v]
            for j in range(8):
                c[j] = c[j] * inv[j]
                for i in range(j + 1, 8):
                    c[i] = c[i] - low[i][j] * c[j]
            for j in range(8):
                sv[v] = sv[v] - c[j] * trow[j]
                ev[v] = ev[v] - c[j] * frow[j]
        out = frow[0]
        for i in range(1, 8):
            out = jnp.where(sub == i, frow[i], out)
        ev[b] = out
    return ev


def dot(a, b, ca, cb):
    return lax.dot_general(a, b, (((ca,), (cb,)), ((), ())), precision=EXACT, preferred_element_type=jnp.float32)


def halves(a):
    hi = a.astype(jnp.bfloat16)
    return hi, (a - hi.astype(jnp.float32)).astype(jnp.bfloat16)


def dot3(a, b, ca, cb):
    def one(x, y):
        return lax.dot_general(x, y, (((ca,), (cb,)), ((), ())), preferred_element_type=jnp.float32)

    return one(a[0], b[0]) + (one(a[0], b[1]) + one(a[1], b[0]))


def product_kernel(pos_ref, f_ref, p_ref, slab_ref, gram_ref, acc_ref):
    piece = pos_ref[0] & 7

    @pl.when(pl.program_id(0) == 0)
    def _():
        acc_ref[...] = jnp.zeros(acc_ref.shape, jnp.float32)

    part = p_ref[0, :, pl.ds(pl.multiple_of(128 * (piece >> 1), 128), 128)].T
    acc_ref[...] += dot3(halves(jnp.concatenate([f_ref[0], part], axis=0)), halves(p_ref[0]), 1, 0)

    @pl.when(pl.program_id(0) == pl.num_programs(0) - 1)
    def _():
        slab_ref[...] = acc_ref[:N]
        gram_ref[...] = acc_ref[pl.ds(pl.multiple_of(N + 64 * (piece & 1), 64), 64), :]


def factor_kernel(pos_ref, *refs):
    add_hbm, m_ref, s_ref, add_ref, sems = refs[8:]
    copies = [pltpu.make_async_copy(add_hbm, add_ref, sems.at[8])]
    for k in range(8):
        at = pl.ds(pl.multiple_of(64 * ((pos_ref[0] & 7) ^ k), 64), 64)
        copies.append(pltpu.make_async_copy(refs[k], s_ref.at[at, :], sems.at[k]))
    for copy in copies:
        copy.start()
    for copy in copies:
        copy.wait()
    s_ref[...] = s_ref[...] + add_ref[...]
    rows = lax.broadcasted_iota(jnp.int32, (8, 128), 0)
    lanes = lax.broadcasted_iota(jnp.int32, (8, 128), 1)
    m_ref[...] = jnp.zeros((N, N), jnp.float32)
    for k in range(4):
        lo = B * k
        hi = lo + B
        sv = [s_ref[lo + 8 * v : lo + 8 * v + 8, lo:hi] for v in range(16)]
        ev = [jnp.where(lanes == rows + 8 * v, 1.0, 0.0).astype(jnp.float32) for v in range(16)]
        mk = jnp.concatenate(factor_block(sv, ev), axis=0)
        if k:
            m_ref[lo:hi, :lo] = dot(mk, m_ref[lo:hi, :lo], 1, 0)
        m_ref[lo:hi, lo:hi] = mk
        if k < 3:
            p = dot(s_ref[hi:, lo:hi], mk, 1, 1)
            s_ref[hi:, hi:] = s_ref[hi:, hi:] - dot(p, p, 1, 1)
            m_ref[hi:, :hi] = m_ref[hi:, :hi] - dot(p, m_ref[lo:hi, :hi], 1, 0)


def join_kernel(pos_ref, *refs):
    for k in range(8):
        refs[8][(pos_ref[0] >> 2) ^ k] = refs[k][...]


def update_kernel(pos_ref, m_hbm, trail_hbm, slab_hbm, *refs):
    panel_ref, out_ref, m_ref, slab_ref, x_ref, trail_ref, sems = refs[4:]
    copies = [pltpu.make_async_copy(slab_hbm, slab_ref, sems.at[4]), pltpu.make_async_copy(m_hbm, m_ref, sems.at[6])]
    for q in range(4):
        copies.append(pltpu.make_async_copy(refs[q], x_ref.at[:, (pos_ref[0] & 3) ^ q], sems.at[q]))
    copies.append(pltpu.make_async_copy(trail_hbm, trail_ref, sems.at[5]))
    for copy in copies:
        copy.start()
    for copy in copies:
        copy.wait()
    inv = halves(m_ref[...])
    panel = dot3(halves(slab_ref[...]), inv, 1, 1)
    panel_ref[...] = panel
    cross = dot3(halves(x_ref[...].reshape(N, N)), inv, 1, 1)
    out_ref[...] = trail_ref[...] - dot3(halves(panel), halves(cross), 1, 1)


def shape(n):
    return jax.ShapeDtypeStruct((n, N), jnp.float32)


def swap(x):
    return lax.all_to_all(x, "scen", split_axis=0, concat_axis=0, tiled=True)


def flip(x, axis, bits):
    n = lax.axis_size(axis)
    return lax.ppermute(x, axis, [(i, i ^ bits) for i in range(n)])


def per_device(factor_rows, panel_factor, pivot_add, trailing):
    groups, depth, _ = panel_factor.shape
    pos = lax.axis_index("rows").astype(jnp.int32).reshape(1)
    slab, gram = pl.pallas_call(
        product_kernel,
        grid=(groups,),
        out_shape=(shape(N), shape(64)),
        in_specs=[
            SMEM,
            pl.BlockSpec((1, N, depth), lambda g: (g, 0, 0)),
            pl.BlockSpec((1, depth, N), lambda g: (g, 0, 0)),
        ],
        out_specs=(pl.BlockSpec((N, N), lambda g: (0, 0)), pl.BlockSpec((64, N), lambda g: (0, 0))),
        scratch_shapes=[pltpu.VMEM((N + 128, N), jnp.float32)],
        compiler_params=pltpu.CompilerParams(vmem_limit_bytes=56 << 20),
        name="product",
    )(pos, factor_rows, panel_factor)

    own = swap(slab.reshape(8, 64, N))
    own = own.sum(0)
    gram = gram + flip(gram, "scen", 1)
    gram = (gram + flip(gram, "scen", 2)) + (flip(gram, "scen", 4) + flip(gram, "scen", 6))
    near = [gram]
    for b in (2, 4, 6):
        near.append(flip(gram, "rows", b))
    far = [flip(x, "rows", 1) for x in near]
    pieces = [x for pair in zip(near, far) for x in pair]
    m = pl.pallas_call(
        factor_kernel,
        out_shape=shape(N),
        in_specs=[SMEM] + [HBM] * 9,
        out_specs=VMEM,
        scratch_shapes=[pltpu.VMEM((N, N), jnp.float32)] * 2 + [pltpu.SemaphoreType.DMA((9,))],
        name="factor",
    )(pos, *pieces, pivot_add)

    column = [own[:16]]
    column += [flip(column[0], "rows", 4 * k) for k in range(1, 8)]
    column = pl.pallas_call(
        join_kernel,
        out_shape=jax.ShapeDtypeStruct((8, 16, N), jnp.float32),
        in_specs=[SMEM] + [VMEM] * 8,
        out_specs=VMEM,
        compiler_params=pltpu.CompilerParams(vmem_limit_bytes=2 << 20),
        name="join",
    )(pos, *column)
    cross = [column] + [flip(column, "rows", q) for q in (1, 2, 3)]
    whole = swap(jnp.broadcast_to(own[None], (8, 64, N))).reshape(N, N)
    return pl.pallas_call(
        update_kernel,
        out_shape=(shape(N), shape(N)),
        in_specs=[SMEM] + [HBM] * 7,
        out_specs=(VMEM, VMEM),
        scratch_shapes=[
            pltpu.VMEM((N, N), jnp.float32),
            pltpu.VMEM((N, N), jnp.float32),
            pltpu.VMEM((8, 4, 16, N), jnp.float32),
            pltpu.VMEM((N, N), jnp.float32),
            pltpu.SemaphoreType.DMA((7,)),
        ],
        compiler_params=pltpu.CompilerParams(vmem_limit_bytes=28 << 20),
        name="update",
    )(pos, m, trailing, whole, *cross)


def solution(mesh):
    return jax.shard_map(
        per_device,
        mesh=mesh,
        in_specs=(P("scen", "rows", None), P("scen", None, None), P(), P("rows", "scen")),
        out_specs=(P("rows", None), P("rows", "scen")),
        check_vma=False,
    )
```

```python
import jax
import jax.numpy as jnp
from jax import lax
from jax.experimental import pallas as pl
from jax.experimental.pallas import tpu as pltpu
from jax.sharding import PartitionSpec as P


N = 512
B = 128
EXACT = lax.Precision.HIGHEST
VMEM = pl.BlockSpec(memory_space=pltpu.VMEM)
HBM = pl.BlockSpec(memory_space=pltpu.HBM)
SMEM = pl.BlockSpec(memory_space=pltpu.SMEM)


def spread(x):
    return jnp.broadcast_to(x, (8, 128))


def factor_block(sv, ev):
    sub = lax.broadcasted_iota(jnp.int32, (8, 128), 0)
    for b in range(16):
        col = {v: [spread(sv[v][:, 8 * b + i : 8 * b + i + 1]) for i in range(8)] for v in range(b, 16)}
        trow = [spread(sv[b][i : i + 1, :]) for i in range(8)]
        frow = [spread(ev[b][i : i + 1, :]) for i in range(8)]
        el = [[spread(col[b][j][i : i + 1, :]) for j in range(i + 1)] for i in range(8)]
        low = [[None] * 8 for _ in range(8)]
        inv = [None] * 8
        for j in range(8):
            inv[j] = lax.rsqrt(el[j][j])
            for i in range(j + 1, 8):
                low[i][j] = el[i][j] * inv[j]
            for i in range(j + 1, 8):
                for m in range(j + 1, i + 1):
                    el[i][m] = el[i][m] - low[i][j] * low[m][j]
            trow[j] = trow[j] * inv[j]
            frow[j] = frow[j] * inv[j]
            for i in range(j + 1, 8):
                trow[i] = trow[i] - low[i][j] * trow[j]
                frow[i] = frow[i] - low[i][j] * frow[j]
        for v in range(b + 1, 16):
            c = col[v]
            for j in range(8):
                c[j] = c[j] * inv[j]
                for i in range(j + 1, 8):
                    c[i] = c[i] - low[i][j] * c[j]
            for j in range(8):
                sv[v] = sv[v] - c[j] * trow[j]
                ev[v] = ev[v] - c[j] * frow[j]
        out = frow[0]
        for i in range(1, 8):
            out = jnp.where(sub == i, frow[i], out)
        ev[b] = out
    return ev


def dot(a, b, ca, cb):
    return lax.dot_general(a, b, (((ca,), (cb,)), ((), ())), precision=EXACT, preferred_element_type=jnp.float32)


def halves(a):
    hi = a.astype(jnp.bfloat16)
    return hi, (a - hi.astype(jnp.float32)).astype(jnp.bfloat16)


def dot3(a, b, ca, cb):
    def one(x, y):
        return lax.dot_general(x, y, (((ca,), (cb,)), ((), ())), preferred_element_type=jnp.float32)

    return one(a[0], b[0]) + (one(a[0], b[1]) + one(a[1], b[0]))


def product_kernel(pos_ref, f_ref, p_ref, first_ref, rest_ref, gram_ref, acc_ref, part_ref):
    piece = pos_ref[0] & 7

    @pl.when(pl.program_id(0) == 0)
    def _():
        acc_ref[...] = jnp.zeros(acc_ref.shape, jnp.float32)

    part_ref[...] = p_ref[0, :, pl.ds(pl.multiple_of(128 * (piece >> 1), 128), 128)].T
    part = part_ref[pl.ds(pl.multiple_of(64 * (piece & 1), 64), 64), :]
    acc_ref[...] += dot3(halves(jnp.concatenate([f_ref[0], part], axis=0)), halves(p_ref[0]), 1, 0)

    @pl.when(pl.program_id(0) == pl.num_programs(0) - 1)
    def _():
        for k in range(8):
            first_ref[k] = acc_ref[64 * k : 64 * k + 16]
            rest_ref[k] = acc_ref[64 * k + 16 : 64 * k + 64]
        gram_ref[...] = acc_ref[N:]


def factor_kernel(pos_ref, *refs):
    add_hbm, m_ref, s_ref, add_ref, sems = refs[8:]
    copies = [pltpu.make_async_copy(add_hbm, add_ref, sems.at[8])]
    for k in range(8):
        at = pl.ds(pl.multiple_of(64 * ((pos_ref[0] & 7) ^ k), 64), 64)
        copies.append(pltpu.make_async_copy(refs[k], s_ref.at[at, :], sems.at[k]))
    for copy in copies:
        copy.start()
    for copy in copies:
        copy.wait()
    s_ref[...] = s_ref[...] + add_ref[...]
    rows = lax.broadcasted_iota(jnp.int32, (8, 128), 0)
    lanes = lax.broadcasted_iota(jnp.int32, (8, 128), 1)
    m_ref[...] = jnp.zeros((N, N), jnp.float32)
    for k in range(4):
        lo = B * k
        hi = lo + B
        sv = [s_ref[lo + 8 * v : lo + 8 * v + 8, lo:hi] for v in range(16)]
        ev = [jnp.where(lanes == rows + 8 * v, 1.0, 0.0).astype(jnp.float32) for v in range(16)]
        mk = jnp.concatenate(factor_block(sv, ev), axis=0)
        if k:
            m_ref[lo:hi, :lo] = dot(mk, m_ref[lo:hi, :lo], 1, 0)
        m_ref[lo:hi, lo:hi] = mk
        if k < 3:
            p = dot(s_ref[hi:, lo:hi], mk, 1, 1)
            s_ref[hi:, hi:] = s_ref[hi:, hi:] - dot(p, p, 1, 1)
            m_ref[hi:, :hi] = m_ref[hi:, :hi] - dot(p, m_ref[lo:hi, :hi], 1, 0)


def join_kernel(pos_ref, *refs):
    for k in range(8):
        refs[8][(pos_ref[0] >> 2) ^ k] = refs[k][...]


def update_kernel(pos_ref, m_hbm, trail_hbm, slab_hbm, *refs):
    panel_ref, out_ref, m_ref, slab_ref, x_ref, trail_ref, sems = refs[4:]
    copies = [pltpu.make_async_copy(slab_hbm, slab_ref, sems.at[4]), pltpu.make_async_copy(m_hbm, m_ref, sems.at[6])]
    for q in range(4):
        copies.append(pltpu.make_async_copy(refs[q], x_ref.at[:, (pos_ref[0] & 3) ^ q], sems.at[q]))
    copies.append(pltpu.make_async_copy(trail_hbm, trail_ref, sems.at[5]))
    for copy in copies:
        copy.start()
    for copy in copies:
        copy.wait()
    inv = halves(m_ref[...])
    panel = dot3(halves(slab_ref[...]), inv, 1, 1)
    panel_ref[...] = panel
    cross = dot3(halves(x_ref[...].reshape(N, N)), inv, 1, 1)
    out_ref[...] = trail_ref[...] - dot3(halves(panel), halves(cross), 1, 1)


def shape(n):
    return jax.ShapeDtypeStruct((n, N), jnp.float32)


def swap(x):
    return lax.all_to_all(x, "scen", split_axis=0, concat_axis=0, tiled=True)


def flip(x, axis, bits):
    n = lax.axis_size(axis)
    return lax.ppermute(x, axis, [(i, i ^ bits) for i in range(n)])


def per_device(factor_rows, panel_factor, pivot_add, trailing):
    groups, depth, _ = panel_factor.shape
    pos = lax.axis_index("rows").astype(jnp.int32).reshape(1)
    first, rest, gram = pl.pallas_call(
        product_kernel,
        grid=(groups,),
        out_shape=(jax.ShapeDtypeStruct((8, 16, N), jnp.float32), jax.ShapeDtypeStruct((8, 48, N), jnp.float32), shape(64)),
        in_specs=[
            SMEM,
            pl.BlockSpec((1, N, depth), lambda g: (g, 0, 0)),
            pl.BlockSpec((1, depth, N), lambda g: (g, 0, 0)),
        ],
        out_specs=(
            pl.BlockSpec((8, 16, N), lambda g: (0, 0, 0)),
            pl.BlockSpec((8, 48, N), lambda g: (0, 0, 0)),
            pl.BlockSpec((64, N), lambda g: (0, 0)),
        ),
        scratch_shapes=[pltpu.VMEM((N + 64, N), jnp.float32), pltpu.VMEM((128, depth), jnp.float32)],
        compiler_params=pltpu.CompilerParams(vmem_limit_bytes=56 << 20),
        name="product",
    )(pos, factor_rows, panel_factor)

    first = swap(first)
    first = lax.optimization_barrier(first.sum(0))
    rest = swap(rest)
    rest = lax.optimization_barrier(rest.sum(0))
    gram = gram + flip(gram, "scen", 1)
    gram = (gram + flip(gram, "scen", 2)) + (flip(gram, "scen", 4) + flip(gram, "scen", 6))
    near = [gram]
    for b in (2, 4, 6):
        near.append(flip(gram, "rows", b))
    far = [flip(x, "rows", 1) for x in near]
    pieces = [x for pair in zip(near, far) for x in pair]
    m = pl.pallas_call(
        factor_kernel,
        out_shape=shape(N),
        in_specs=[SMEM] + [HBM] * 9,
        out_specs=VMEM,
        scratch_shapes=[pltpu.VMEM((N, N), jnp.float32)] * 2 + [pltpu.SemaphoreType.DMA((9,))],
        name="factor",
    )(pos, *pieces, pivot_add)

    column = [first]
    column += [flip(column[0], "rows", 4 * k) for k in range(1, 8)]
    column = pl.pallas_call(
        join_kernel,
        out_shape=jax.ShapeDtypeStruct((8, 16, N), jnp.float32),
        in_specs=[SMEM] + [VMEM] * 8,
        out_specs=VMEM,
        compiler_params=pltpu.CompilerParams(vmem_limit_bytes=2 << 20),
        name="join",
    )(pos, *column)
    cross = [column] + [flip(column, "rows", q) for q in (1, 2, 3)]
    own = jnp.concatenate([first, rest], axis=0)
    whole = swap(jnp.broadcast_to(own[None], (8, 64, N))).reshape(N, N)
    return pl.pallas_call(
        update_kernel,
        out_shape=(shape(N), shape(N)),
        in_specs=[SMEM] + [HBM] * 7,
        out_specs=(VMEM, VMEM),
        scratch_shapes=[
            pltpu.VMEM((N, N), jnp.float32),
            pltpu.VMEM((N, N), jnp.float32),
            pltpu.VMEM((8, 4, 16, N), jnp.float32),
            pltpu.VMEM((N, N), jnp.float32),
            pltpu.SemaphoreType.DMA((7,)),
        ],
        compiler_params=pltpu.CompilerParams(vmem_limit_bytes=28 << 20),
        name="update",
    )(pos, m, trailing, whole, *cross)


def solution(mesh):
    return jax.shard_map(
        per_device,
        mesh=mesh,
        in_specs=(P("scen", "rows", None), P("scen", None, None), P(), P("rows", "scen")),
        out_specs=(P("rows", None), P("rows", "scen")),
        check_vma=False,
    )
```
